512 devices in a mesh: dp: 32 (over z, core), vocab: 16 (over y, x).
Axes of the slice: x: 4, y: 4, z: 16, core: 2. Of those that a mesh axis runs over, the one named last changes fastest.
Arguments:
- hidden: bfloat16 [2, 32, 128, 2048], P(None, 'dp'), may hold values from -320 to 320
- out_weight: bfloat16 [2048, 51200], P('dp', 'vocab'), may hold values from -1 to 1
- targets: int32 [2, 32, 128], P(None, 'dp'), may hold values from 0 to 51199
- prompt_start: int32 [2, 32], P(None, 'dp'), may hold values from 0 to 31
- response_len: int32 [2, 32], P(None, 'dp'), may hold values from 16 to 80, as said below
- partner: int32 [2, 32], P(None, 'dp'), may hold values from 0 to 31, as said below
- ref_scores: float32 [2, 32], P(None, 'dp'), may hold values from -60 to 60
Outputs:
- pair_loss: float32 [2, 32], P(None, 'dp')
- grad_hidden: float32 [2, 32, 128, 2048], P(None, 'dp', None, 'vocab')
The draws below stay inside these ranges and needn't reach their ends.
Inputs may be any that keep to these rules, and one draw needn't show every extreme that they name: In each microbatch partner pairs the sequences: the partner of the partner of s is s, and it differs from s. `response_len`: the response length of sequence s is below 17 + 64 * (s + 1) // 32.
All inputs are finite; a program needn't handle non-finite values.
Results may differ from the reference program's by a relative error of at most 0.0059.
Values may be sent and summed in bfloat16 or wider, within the bound.
A program may use at most 64 MiB of HBM per device.

```python
import math
import jax
import jax.numpy as jnp
import numpy as np
from jax import lax

D = 2048
VOC = 51200
MB = 2
L = 128
SEQS = 32


def common_direction(key):
    shared = jax.random.normal(jax.random.fold_in(key, 9173), (D,), jnp.float32)
    return jnp.clip(shared, -4.0, 4.0) / jnp.sqrt(jnp.float32(D))


def draw_out_weight(key, part):
    direction = common_direction(key)
    noise = jax.random.normal(jax.random.fold_in(key, 4421), (D, VOC), jnp.float32)
    values = jnp.clip(noise, -4.0, 4.0) / jnp.sqrt(jnp.float32(D)) + direction[:, None]
    return values.astype(jnp.bfloat16)


def draw_hidden(key, part):
    direction = common_direction(key)
    key_base = jax.random.fold_in(key, 11)
    key_row = jax.random.fold_in(key, 15)
    key_shift = jax.random.fold_in(key, 16)
    values = jax.random.normal(key_base, (MB, SEQS, L, D), jnp.float32)
    shift_row = jax.random.randint(key_row, (MB, SEQS, 1), 0, L)
    position = jnp.arange(L, dtype=jnp.int32)[None, None, :]
    shift_levels = jnp.array([120.0, 200.0, 280.0], jnp.float32)
    shift = shift_levels[jax.random.randint(key_shift, (MB, SEQS, 1), 0, 3)]
    shift = jnp.where(position == shift_row, shift, 0.0)
    unit = direction / jnp.sum(direction * direction)
    values = values + shift[..., None] * unit[None, None, None, :]
    return jnp.clip(values, -320.0, 320.0).astype(jnp.bfloat16)


def draw_response_len(key, part):
    lowest = L // 8
    index = jnp.arange(SEQS, dtype=jnp.int32)
    upper_end = lowest + 1 + L // 2 * (index + 1) // SEQS
    lengths = jax.random.randint(key, (MB, SEQS), lowest, upper_end[None, :], dtype=jnp.int32)
    lengths = lengths.at[0, SEQS - 1].set(jnp.int32(lowest + L // 2))
    return lengths.at[0, 0].set(jnp.int32(lowest))


def draw_partner(key, part):

    def one_batch(batch_key):
        order = jax.random.permutation(batch_key, SEQS).astype(jnp.int32)
        paired = jnp.zeros((SEQS,), jnp.int32)
        paired = paired.at[order[0::2]].set(order[1::2])
        return paired.at[order[1::2]].set(order[0::2])
    return jax.vmap(one_batch)(jax.random.split(key, MB))


def place_ends(result, stream_key, low, largest):
    longest = result.shape.index(max(result.shape))
    spots = []
    for shift in (0, 1):
        where = [jax.random.randint(jax.random.fold_in(stream_key, axis), (), 0, length) for axis, length in enumerate(result.shape)]
        where[longest] = (where[longest] + shift) % result.shape[longest]
        spots.append(tuple(where))
    return result.at[spots[0]].set(low).at[spots[1]].set(largest)


def level_of(stream_key, dims, shards, smallest, high):
    def one(axis_at, shards_of):
        steps = jax.random.uniform(jax.random.fold_in(jax.random.fold_in(stream_key, 6), axis_at), (shards_of,), jnp.float32, smallest / len(shards), high / len(shards))
        return jnp.repeat(jnp.exp(steps), dims[axis_at] // shards_of).reshape((-1,) + (1,) * (len(dims) - axis_at - 1))

    gain = one(*shards[0])
    for cut in shards[1:]:
        gain = gain * one(*cut)
    return gain


def rank_table(amount, lean):
    portions = [(1 << 20) // math.isqrt(grade ** lean) + 1 for grade in range(1, amount + 1)]
    width = 1 + sum(portions) // (1 << 30)
    return np.cumsum(np.array([max(1, weight // width) for weight in portions]))


def ranked_ids(own_key, dims, amount, skew):
    grid = rank_table(amount, skew)
    ticket = jax.random.randint(jax.random.fold_in(own_key, 1), dims, 0, int(grid[amount - 1]))
    grade = jnp.searchsorted(jnp.asarray(grid, jnp.int32), ticket, side="right")
    return jax.random.permutation(jax.random.fold_in(own_key, 2), amount)[grade].astype(jnp.int32)


def gaussian(stream_key, shape, scale, most, shards=(), kind=jnp.bfloat16):
    result = scale * jax.random.normal(stream_key, shape, jnp.float32)
    if shards:
        result = result * level_of(stream_key, shape, shards, -0.22, 0.18)
    return jnp.clip(result, -most, most).astype(kind)


def setup_inputs(seed: int = 0) -> dict:
    streams_of = jax.random.split(jax.random.key(seed), 8)
    hidden = draw_hidden(jax.random.fold_in(streams_of[7], 71), 0)
    out_weight = draw_out_weight(jax.random.fold_in(streams_of[7], 71), 0)
    targets = place_ends(ranked_ids(streams_of[2], (MB, SEQS, L), VOC, 2), jax.random.fold_in(streams_of[2], 3), 0, VOC - 1).astype(jnp.int32)
    prompt_start = place_ends(jax.random.randint(streams_of[3], (MB, SEQS), 0, L // 4), jax.random.fold_in(streams_of[3], 1), 0, (L // 4) - 1).astype(jnp.int32)
    response_len = draw_response_len(jax.random.fold_in(streams_of[7], 71), 0)
    partner = draw_partner(jax.random.fold_in(streams_of[7], 71), 0)
    ref_scores = gaussian(streams_of[6], (MB, SEQS), 10.0, 60.0, ((1, 32),), jnp.float32)
    return {"hidden": hidden, "out_weight": out_weight, "targets": targets, "prompt_start": prompt_start, "response_len": response_len, "partner": partner, "ref_scores": ref_scores}


margin_beta = 0.1
loss_scale = 65536.0


def reference(hidden, out_weight, targets, prompt_start, response_len, partner, ref_scores):
    weight_wide = out_weight.astype(jnp.float32)
    flat_hidden = hidden.reshape(MB * SEQS, L, D)
    flat_targets = targets.reshape(MB * SEQS, L)
    position = jnp.arange(L, dtype=jnp.int32)
    first_pos = prompt_start.reshape(MB * SEQS, 1)
    end_pos = (prompt_start + response_len).reshape(MB * SEQS, 1)
    response_mask = ((position[None, :] >= first_pos) & (position[None, :] < end_pos)).astype(jnp.float32)
    vocab_ids = jnp.arange(VOC, dtype=jnp.int32)

    def seq_logits(seq_hidden):
        return jnp.dot(seq_hidden.astype(jnp.float32), weight_wide, precision=lax.Precision.HIGHEST)

    def forward(element):
        seq_hidden, seq_targets = element
        logits = seq_logits(seq_hidden)
        row_peak = jnp.max(logits, axis=1)
        log_total = row_peak + jnp.log(jnp.sum(jnp.exp(logits - row_peak[:, None]), axis=1))
        picked = jnp.sum(jnp.where(seq_targets[:, None] == vocab_ids[None, :], logits, 0.0), axis=1)
        return picked - log_total, log_total

    token_logp, log_total = lax.map(forward, (flat_hidden, flat_targets))
    seq_sum = jnp.sum(response_mask * token_logp, axis=1).reshape(MB, SEQS)
    mean_length = jnp.sum(response_len).astype(jnp.float32) / (MB * SEQS)
    score_gap = seq_sum / mean_length - ref_scores
    partner_gap = jnp.take_along_axis(score_gap, partner, axis=1)
    seq_index = jnp.arange(SEQS, dtype=jnp.int32)
    pair_sign = jnp.where(seq_index[None, :] < partner, 1.0, -1.0)
    margin = margin_beta * pair_sign * (score_gap - partner_gap)
    pair_loss = jax.nn.softplus(-margin)
    seq_weight = -loss_scale * margin_beta * pair_sign * jax.nn.sigmoid(-margin) / mean_length
    row_weight = seq_weight.reshape(MB * SEQS, 1) * response_mask

    def backward(element):
        seq_hidden, seq_targets, seq_total, seq_rows = element
        logits = seq_logits(seq_hidden)
        softmax = jnp.exp(logits - seq_total[:, None])
        onehot = (seq_targets[:, None] == vocab_ids[None, :]).astype(jnp.float32)
        grad_logits = (seq_rows[:, None] * (onehot - softmax)).astype(jnp.bfloat16)
        return jnp.dot(grad_logits.astype(jnp.float32), weight_wide.T, precision=lax.Precision.HIGHEST)

    grad_hidden = lax.map(backward, (flat_hidden, flat_targets, log_total, row_weight))
    return pair_loss, grad_hidden.reshape(MB, SEQS, L, D)
```

```python
import functools

import jax
import jax.numpy as jnp
from jax import lax
from jax.experimental import pallas as pl
from jax.experimental.pallas import tpu as pltpu
from jax.sharding import PartitionSpec as P

MESH = pl.DeviceIdType.MESH
margin_beta = 0.1
loss_scale = 65536.0
window = 80
chunk_rows = 16


def kernel(
    dp_n, nv, h_ref, w_hbm, t_ref, start_ref, len_ref, partner_ref, refs_ref,
    loss_ref, grad_ref,
    wg, hc, logits, gl, stat, gsend, grecv, msg,
    own_sem, ring_s, ring_r, sib_s, sib_r, stat_s, stat_r, msg_s, msg_r, g_s, g_r,
):
    dp, v = lax.axis_index("dp"), lax.axis_index("vocab")
    nz, steps = dp_n // 2, dp_n // 4
    z = dp // 2
    sib_id = dp + 1 - 2 * lax.rem(dp, 2)
    kr, cols = w_hbm.shape
    depth = hc.shape[1]
    dcol = depth // nv
    nc = kr // chunk_rows
    ck = 2 * kr
    rows_n = 2 * window
    ncol = cols // 5
    f32, bf16 = jnp.float32, jnp.bfloat16

    def rows(owner, j):
        return pl.ds(pl.multiple_of(owner * kr + j * chunk_rows, chunk_rows), chunk_rows)

    own_rows = pl.ds(pl.multiple_of(dp * kr, kr), kr)
    own_copy = pltpu.make_async_copy(w_hbm, wg.at[own_rows], own_sem)
    own_copy.start()

    bar = pltpu.get_barrier_semaphore()

    @pl.loop(1, dp_n)
    def _(k):
        pl.semaphore_signal(bar, inc=1, device_id=(lax.rem(dp + k, dp_n), v), device_id_type=MESH)

    @pl.loop(1, nv)
    def _(k):
        pl.semaphore_signal(bar, inc=1, device_id=(dp, lax.rem(v + k, nv)), device_id_type=MESH)

    own_copy.wait()
    pl.semaphore_wait(bar, dp_n - 1 + nv - 1)

    def owner_of(d, h):
        back = (dp_n - 2) * h if d == 0 else 2 * h
        return lax.rem(dp + back, dp_n)

    def ring(d, h, j, owner):
        to = lax.rem(dp + (2 if d == 0 else dp_n - 2), dp_n)
        return pltpu.make_async_remote_copy(
            src_ref=wg.at[rows(owner, j)], dst_ref=wg.at[rows(owner, j)],
            send_sem=ring_s.at[d, h, j], recv_sem=ring_r.at[d, h, j],
            device_id=(to, v), device_id_type=MESH,
        )

    def send(d, h, j):
        return ring(d, h, j, owner_of(d, h))

    def arrived(d, h, j):
        ring(d, h, j, owner_of(d, h + 1)).wait_recv()

    def sib(d, h, j, owner):
        return pltpu.make_async_remote_copy(
            src_ref=wg.at[rows(owner, j)], dst_ref=wg.at[rows(owner, j)],
            send_sem=sib_s.at[d, h, j], recv_sem=sib_r.at[d, h, j],
            device_id=(sib_id, v), device_id_type=MESH,
        )

    def twin(owner):
        return owner + 1 - 2 * lax.rem(owner, 2)

    for j in range(nc):
        for d in (0, 1):
            send(d, 0, j).start()
    for j in range(nc):
        sib(0, steps, j, dp).start()

    starts = [start_ref[m : m + 1, 0:1] for m in (0, 1)]
    lens = [len_ref[m : m + 1, 0:1] for m in (0, 1)]
    tcols, masks = [], []
    for m in (0, 1):
        pos = lax.broadcasted_iota(jnp.int32, (window, 128), 1)
        row = lax.broadcasted_iota(jnp.int32, (window, 128), 0)
        pick = pos == row + starts[m]
        pick_f = pick.astype(f32)
        tcols.append(jnp.sum(pick_f * t_ref[m : m + 1, :].astype(f32), axis=1, keepdims=True))
        rowc = lax.broadcasted_iota(jnp.int32, (window, 1), 0)
        masks.append((rowc < lens[m]).astype(f32))
        sel = pick_f.astype(bf16)

        @pl.loop(0, depth // 512)
        def _(c):
            at = pl.ds(pl.multiple_of(c * 512, 512), 512)
            got = jnp.dot(sel, h_ref[m * 128 : m * 128 + 128, at], preferred_element_type=f32)
            hc[m * window : (m + 1) * window, at] = got.astype(bf16)

    local_t = jnp.concatenate(tcols, axis=0) - (v * cols).astype(f32)

    def chip_rows(zz):
        return pl.ds(pl.multiple_of(zz * ck, ck), ck)

    def accumulate(zs, first):
        hs = [hc[:, chip_rows(zz)] for zz in zs]
        lhs = hs[0] if len(hs) == 1 else jnp.concatenate(hs, axis=1)

        @pl.loop(0, cols // ncol)
        def _(c):
            at = pl.ds(pl.multiple_of(c * ncol, 128), ncol)
            ws = [wg[chip_rows(zz), at] for zz in zs]
            rhs = ws[0] if len(ws) == 1 else jnp.concatenate(ws, axis=0)
            got = jnp.dot(lhs, rhs, preferred_element_type=f32)
            if first:
                logits[:, at] = got
            else:
                logits[:, at] += got

    half = nc // 2
    full_js = (tuple(range(nc)), tuple(range(nc)))
    half_js = (tuple(range(half)), tuple(range(half, nc)))

    def relay(h, js, forward):
        for j in range(nc):
            for d in (0, 1):
                if j in js[d]:
                    arrived(d, h, j)
                    if j in forward[d]:
                        send(d, h + 1, j).start()
                    sib(d, h, j, owner_of(d, h + 1)).start()

    def compute(h):
        for j in range(nc):
            for d in (0, 1):
                sib(d, h, j, twin(owner_of(d, h + 1))).wait_recv()
        accumulate((lax.rem(z + nz - h - 1, nz), lax.rem(z + h + 1, nz)), False)

    for j in range(nc):
        sib(0, steps, j, sib_id).wait_recv()
    accumulate((z,), True)

    none = ((), ())

    @pl.loop(0, steps - 2)
    def _(h):
        relay(h, full_js, full_js)

        @pl.when(h > 0)
        def _():
            compute(h - 1)

    if steps > 2:
        relay(steps - 2, full_js, half_js)
        compute(steps - 3)
    else:
        relay(0, full_js, half_js)
    relay(steps - 1, half_js, none)
    compute(steps - 2)
    for d in (0, 1):
        for j in half_js[d]:
            sib(d, steps - 1, j, twin(owner_of(d, steps))).wait_recv()
    accumulate((lax.rem(z + steps, nz),), False)

    nt = cols // ncol

    def ids(c):
        at = lax.broadcasted_iota(jnp.int32, (1, ncol), 1) + c * ncol
        return at.astype(f32)

    def cut(c):
        return pl.ds(pl.multiple_of(c * ncol, 128), ncol)

    peak = lax.fori_loop(
        0, nt,
        lambda c, m: jnp.maximum(m, jnp.max(logits[:, cut(c)], axis=1, keepdims=True)),
        jnp.full((rows_n, 1), -jnp.inf, f32),
    )

    def tally(c, carry):
        total, target = carry
        part = logits[:, cut(c)]
        total = total + jnp.sum(jnp.exp(part - peak), axis=1, keepdims=True)
        target = target + jnp.sum(jnp.where(local_t == ids(c), part, 0.0), axis=1, keepdims=True)
        return total, target

    zero = jnp.zeros((rows_n, 1), f32)
    total, target = lax.fori_loop(0, nt, tally, (zero, zero))
    lane = lax.broadcasted_iota(jnp.int32, (rows_n, 128), 1)
    table = jnp.where(lane == 0, peak, jnp.where(lane == 1, total, jnp.where(lane == 2, target, 0.0)))
    table = jnp.concatenate([table, jnp.zeros((256 - rows_n, 128), f32)], axis=0)
    stat[v] = jnp.transpose(table)[0:8, :]

    def stat_copy(peer, slot):
        return pltpu.make_async_remote_copy(
            src_ref=stat.at[slot], dst_ref=stat.at[slot],
            send_sem=stat_s.at[peer], recv_sem=stat_r.at[slot],
            device_id=(dp, peer), device_id_type=MESH,
        )

    @pl.loop(1, nv)
    def _(k):
        stat_copy(lax.rem(v + k, nv), v).start()

    @pl.loop(1, nv)
    def _(k):
        peer = lax.rem(v + k, nv)
        stat_copy(peer, peer).wait_recv()

    top = stat[0, 0:1, :]
    for k in range(1, nv):
        top = jnp.maximum(top, stat[k, 0:1, :])
    whole = jnp.zeros_like(top)
    hit = jnp.zeros_like(top)
    for k in range(nv):
        whole = whole + stat[k, 1:2, :] * jnp.exp(stat[k, 0:1, :] - top)
        hit = hit + stat[k, 2:3, :]
    log_total = top + jnp.log(whole)
    token = hit - log_total
    spot = lax.broadcasted_iota(jnp.int32, (1, 256), 1)
    sums = []
    for m in (0, 1):
        inside = (spot >= m * window) & (spot < m * window + lens[m])
        sums.append(jnp.sum(jnp.where(inside, token, 0.0), axis=1, keepdims=True))

    refs = [refs_ref[m : m + 1, 0:1] for m in (0, 1)]
    count = (lens[0] + lens[1]).astype(f32)
    ml = lax.broadcasted_iota(jnp.int32, (8, 128), 1)
    mr = lax.broadcasted_iota(jnp.int32, (8, 128), 0)
    word = jnp.zeros((8, 128), f32)
    for at, value in enumerate((sums[0], sums[1], refs[0], refs[1], count)):
        word = jnp.where((ml == at) & (mr == 0), value, word)
    msg[dp] = word

    def msg_copy(peer, slot):
        return pltpu.make_async_remote_copy(
            src_ref=msg.at[slot], dst_ref=msg.at[slot],
            send_sem=msg_s.at[peer], recv_sem=msg_r.at[slot],
            device_id=(peer, v), device_id_type=MESH,
        )

    @pl.loop(1, dp_n)
    def _(k):
        msg_copy(lax.rem(dp + k, dp_n), dp).start()

    lt_col = jnp.transpose(jnp.broadcast_to(log_total, (128, 256)))[0:rows_n, 0:1]

    @pl.loop(0, nt)
    def _(c):
        soft = jnp.exp(logits[:, cut(c)] - lt_col)
        onehot = (local_t == ids(c)).astype(f32)
        gl[:, cut(c)] = (onehot - soft).astype(bf16)

    def g_copy(peer, slot):
        return pltpu.make_async_remote_copy(
            src_ref=gsend.at[peer], dst_ref=grecv.at[slot],
            send_sem=g_s.at[peer], recv_sem=g_r.at[slot],
            device_id=(dp, peer), device_id_type=MESH,
        )

    npair = nv // 2

    @pl.loop(0, npair)
    def _(i):
        q = lax.rem(v // 2 + i + 1, npair)
        at = pl.ds(pl.multiple_of(q * 2 * dcol, 128), 2 * dcol)
        got = lax.dot_general(
            gl[...], wg[at, :], (((1,), (1,)), ((), ())), preferred_element_type=f32
        ).astype(bf16)
        for side in (0, 1):
            peer = 2 * q + side
            gsend[peer] = got[:, side * dcol : (side + 1) * dcol]

            @pl.when(peer != v)
            def _():
                g_copy(peer, v).start()

    @pl.loop(1, dp_n)
    def _(k):
        peer = lax.rem(dp + k, dp_n)
        msg_copy(peer, peer).wait_recv()

    board = jnp.sum(msg[...], axis=1)
    mean_length = jnp.sum(board[:, 4:5], axis=0, keepdims=True) / float(2 * dp_n)
    who = lax.broadcasted_iota(jnp.int32, (dp_n, 1), 0)
    weights = []
    loss_lane = lax.broadcasted_iota(jnp.int32, (8, 128), 0)
    losses = jnp.zeros((8, 128), f32)
    for m in (0, 1):
        gaps = board[:, m : m + 1] / mean_length - board[:, 2 + m : 3 + m]
        own_gap = sums[m] / mean_length - refs[m]
        partner = partner_ref[m : m + 1, 0:1]
        partner_gap = jnp.sum(jnp.where(who == partner, gaps, 0.0), axis=0, keepdims=True)
        sign = jnp.where(dp < partner, 1.0, -1.0)
        margin = margin_beta * sign * (own_gap - partner_gap)
        small = jnp.exp(-jnp.abs(margin))
        loss = jnp.maximum(-margin, 0.0) + jnp.log1p(small)
        sig = jnp.where(margin >= 0, small, 1.0) / (1.0 + small)
        weights.append(-loss_scale * margin_beta * sign * sig / mean_length)
        losses = jnp.where(loss_lane == m, loss, losses)
    loss_ref[...] = losses

    @pl.loop(1, nv)
    def _(k):
        peer = lax.rem(v + k, nv)
        g_copy(peer, peer).wait_recv()

    summed = lax.fori_loop(
        1, nv,
        lambda k, acc: acc + grecv[lax.rem(v + k, nv)].astype(f32),
        gsend[v].astype(f32),
    )
    for m in (0, 1):
        part = summed[m * window : (m + 1) * window] * (masks[m] * weights[m])
        pos = lax.broadcasted_iota(jnp.int32, (128, window), 0)
        row = lax.broadcasted_iota(jnp.int32, (128, window), 1)
        back = (pos == row + starts[m]).astype(f32)
        grad_ref[m] = jnp.dot(
            back, part, preferred_element_type=f32, precision=lax.Precision.HIGHEST
        )

    @pl.loop(1, nv)
    def _(k):
        peer = lax.rem(v + k, nv)
        stat_copy(peer, v).wait_send()
        g_copy(peer, v).wait_send()

    @pl.loop(1, dp_n)
    def _(k):
        msg_copy(lax.rem(dp + k, dp_n), dp).wait_send()

    @pl.loop(0, steps - 1)
    def _(h):
        for j in range(nc):
            for d in (0, 1):
                send(d, h, j).wait_send()
                sib(d, h, j, owner_of(d, h + 1)).wait_send()

    for d in (0, 1):
        for j in half_js[d]:
            send(d, steps - 1, j).wait_send()
            sib(d, steps - 1, j, owner_of(d, steps)).wait_send()
    for j in range(nc):
        sib(0, steps, j, dp).wait_send()


def solution(mesh):
    dp_n, nv = mesh.shape["dp"], mesh.shape["vocab"]
    steps = dp_n // 4

    def body(hidden, out_weight, targets, prompt_start, response_len, partner, ref_scores):
        micro, seqs, length, depth = hidden.shape
        kr, cols = out_weight.shape
        nc = kr // chunk_rows
        rows_n = 2 * window
        dcol = depth // nv
        f32, bf16 = jnp.float32, jnp.bfloat16
        vm = pl.BlockSpec(memory_space=pltpu.VMEM)
        dma = pltpu.SemaphoreType.DMA
        loss, grad = pl.pallas_call(
            functools.partial(kernel, dp_n, nv),
            out_shape=(
                jax.ShapeDtypeStruct((8, 128), f32),
                jax.ShapeDtypeStruct((micro, length, dcol), f32),
            ),
            in_specs=[vm, pl.BlockSpec(memory_space=pl.ANY), vm, vm, vm, vm, vm],
            out_specs=(vm, vm),
            scratch_shapes=[
                pltpu.VMEM((depth, cols), bf16),
                pltpu.VMEM((rows_n, depth), bf16),
                pltpu.VMEM((rows_n, cols), f32),
                pltpu.VMEM((rows_n, cols), bf16),
                pltpu.VMEM((nv, 8, 256), f32),
                pltpu.VMEM((nv, rows_n, dcol), bf16),
                pltpu.VMEM((nv, rows_n, dcol), bf16),
                pltpu.VMEM((dp_n, 8, 128), f32),
                dma,
                dma((2, steps, nc)),
                dma((2, steps, nc)),
                dma((2, steps + 1, nc)),
                dma((2, steps + 1, nc)),
                dma((nv,)), dma((nv,)),
                dma((dp_n,)), dma((dp_n,)),
                dma((nv,)), dma((nv,)),
            ],
            compiler_params=pltpu.CompilerParams(
                collective_id=0, has_side_effects=True, vmem_limit_bytes=48 * 1024 * 1024
            ),
        )(
            hidden.reshape(micro * length, depth),
            out_weight,
            targets.reshape(micro, length),
            prompt_start,
            response_len,
            partner,
            ref_scores,
        )
        return loss[0:2, 0:1], grad.reshape(micro, seqs, length, dcol)

    return jax.shard_map(
        body,
        mesh=mesh,
        in_specs=(
            P(None, "dp", None, None),
            P("dp", "vocab"),
            P(None, "dp", None),
            P(None, "dp"),
            P(None, "dp"),
            P(None, "dp"),
            P(None, "dp"),
        ),
        out_specs=(P(None, "dp"), P(None, "dp", None, "vocab")),
        check_vma=False,
    )
```

```python
import functools

import jax
import jax.numpy as jnp
from jax import lax
from jax.experimental import pallas as pl
from jax.experimental.pallas import tpu as pltpu
from jax.sharding import PartitionSpec as P

MESH = pl.DeviceIdType.MESH
margin_beta = 0.1
loss_scale = 65536.0
window = 80
groups = 2
spread_at = 2
begin_at = 4


def kernel(
    dp_n, nv, h_hbm, w_hbm, t_hbm, start_hbm, len_hbm, partner_hbm, refs_hbm,
    loss_ref, grad_ref,
    h_ref, t_ref, start_ref, len_ref, partner_ref, refs_ref,
    wt, hall, hx, tg, logits, gl, stat, zstat, gsend, grecv, fsend, frecv, msg,
    in_sem, own_sem, ring_s, ring_r, sib_s, sib_r, hx_s, hx_r, tg_s, tg_r, hb_s, hb_r,
    zst_s, zst_r, stat_s, stat_r, msg_s, msg_r, g_s, g_r, f_s, f_r,
):
    f32, bf16 = jnp.float32, jnp.bfloat16
    dp, v = lax.axis_index("dp"), lax.axis_index("vocab")
    nz = dp_n // 2
    z, core = lax.div(dp, 2), lax.rem(dp, 2)
    sib_id = dp + 1 - 2 * core
    kr, cols = w_hbm.shape
    depth = hall.shape[2]
    dcol = depth // nv
    nt = cols // 128
    arc = nz // groups
    far = (nz - arc) // 2
    seg = 2 * window
    rows_n = groups * seg
    ck = 2 * kr
    lanes = zstat.shape[2]
    kz, zlow = lax.div(z, arc), lax.rem(z, arc)

    inputs = [
        pltpu.make_async_copy(src, dst, in_sem.at[k])
        for k, (src, dst) in enumerate((
            (h_hbm, h_ref), (t_hbm, t_ref), (start_hbm, start_ref), (len_hbm, len_ref),
            (partner_hbm, partner_ref), (refs_hbm, refs_ref),
        ))
    ]
    for copy in inputs:
        copy.start()

    def first_tile(p):
        return lax.div(nt * p + nz - 1, nz)

    base = z + 2 * nz - arc + 1
    tile_base = first_tile(base)
    tile_lo = lax.rem(tile_base, nt)
    n_mine = first_tile(base + arc) - tile_base

    def rows_of(owner):
        return pl.ds(pl.multiple_of(owner * kr, kr), kr)

    def own_copy(t):
        at = pl.ds(pl.multiple_of(t * 128, 128), 128)
        slot = lax.rem(t + nt - tile_lo, nt)
        return pltpu.make_async_copy(w_hbm.at[:, at], wt.at[slot, rows_of(dp)], own_sem.at[t])

    @pl.loop(0, nt)
    def _(t):
        own_copy(t).start()

    bar = pltpu.get_barrier_semaphore()

    @pl.loop(1, dp_n)
    def _(k):
        pl.semaphore_signal(bar, inc=1, device_id=(lax.rem(dp + k, dp_n), v), device_id_type=MESH)

    @pl.loop(1, nv)
    def _(k):
        pl.semaphore_signal(bar, inc=1, device_id=(dp, lax.rem(v + k, nv)), device_id_type=MESH)

    for copy in inputs:
        copy.wait()

    def seg_rows(k):
        return pl.ds(pl.multiple_of(k * seg, 16), seg)

    starts = [start_ref[0:1, m : m + 1] for m in (0, 1)]
    lens = [len_ref[0:1, m : m + 1] for m in (0, 1)]
    tcols, masks = [], []
    for m in (0, 1):
        pos = lax.broadcasted_iota(jnp.int32, (window, 128), 1)
        row = lax.broadcasted_iota(jnp.int32, (window, 128), 0)
        pick_f = (pos == row + starts[m]).astype(f32)
        tcols.append(jnp.sum(pick_f * t_ref[m : m + 1, :].astype(f32), axis=1, keepdims=True))
        masks.append(lax.broadcasted_iota(jnp.int32, (window, 1), 0) < lens[m])
        sel = pick_f.astype(bf16)

        @pl.loop(0, depth // 512)
        def _(c):
            at = pl.ds(pl.multiple_of(c * 512, 512), 512)
            got = jnp.dot(sel, h_ref[m * 128 : m * 128 + 128, at], preferred_element_type=f32)
            hall[2 * kz + m, :, at] = got.astype(bf16)

    tcol = jnp.concatenate(tcols + [jnp.zeros((256 - seg, 1), f32)], axis=0)
    tg[kz] = jnp.transpose(jnp.broadcast_to(tcol, (256, 128)))[0:8, :]

    @pl.loop(0, nt)
    def _(t):
        own_copy(t).wait()

    pl.semaphore_wait(bar, dp_n - 1 + nv - 1)

    def tall(k):
        s = 2 * (zlow + k * arc) + core
        return lax.div(31 + lax.div(64 * (s + 1), dp_n), 16)

    def by_rows(k, act):
        for size in (2, 3, 4, 5):
            pl.when(tall(k) == size)(functools.partial(act, 16 * size))

    def plane_dev(k):
        return 2 * (zlow + k * arc) + core

    mine = pl.ds(pl.multiple_of(v * dcol, 128), dcol)

    def both(k, size):
        return pl.ds(2 * k, 2), pl.ds(0, size)

    def hx_copy(slot, size, to):
        return pltpu.make_async_remote_copy(
            src_ref=hall.at[(*both(slot, size), mine)], dst_ref=hx.at[both(slot, size)],
            send_sem=hx_s.at[to], recv_sem=hx_r.at[slot],
            device_id=(plane_dev(to), v), device_id_type=MESH,
        )

    def tg_copy(slot, to):
        return pltpu.make_async_remote_copy(
            src_ref=tg.at[slot], dst_ref=tg.at[slot],
            send_sem=tg_s.at[to], recv_sem=tg_r.at[slot],
            device_id=(plane_dev(to), v), device_id_type=MESH,
        )

    others = [lax.rem(kz + k, groups) for k in range(1, groups)]
    for to in others:
        by_rows(kz, lambda size: hx_copy(kz, size, to).start())
        tg_copy(kz, to).start()

    sizes = range(nt // nz, -(-nt // nz) + 1)

    def by_tiles(x, act):
        t0 = first_tile(x)
        n = first_tile(x + 1) - t0
        for size in sizes:
            pl.when(n == size)(functools.partial(act, t0 - tile_base, size))

    def ring(d, p, e, src, dst, size, owner, step):
        to = lax.rem(dp + 2 * step, dp_n)
        at = rows_of(owner)
        return pltpu.make_async_remote_copy(
            src_ref=wt.at[pl.ds(src, size), at], dst_ref=wt.at[pl.ds(dst, size), at],
            send_sem=ring_s.at[d, p, e], recv_sem=ring_r.at[d, p, e],
            device_id=(to, v), device_id_type=MESH,
        )

    ahead = (first_tile(base + 1) - tile_base, first_tile(base - 1) - tile_base)

    def place(d, p):
        return base + arc - 1 - p if d == 0 else base + p

    def owner_at(d, e):
        return 2 * lax.rem(z + (nz - e if d == 0 else e), nz) + core

    def direct(d, e, act):
        if d == 0:
            shift = first_tile(base + e) - tile_base
            by_tiles(base + e + arc - 1, lambda src, size: act(
                ring(0, 0, e, src, src - shift, size, dp, e)))
        else:
            by_tiles(base + nz - e, lambda src, size: act(
                ring(1, 0, e, src, 0, size, dp, nz - e)))

    def onward(d, p, e, act):
        owner = owner_at(d, e - 1)
        by_tiles(place(d, p), lambda src, size: act(
            ring(d, p + 1, e, src, src - ahead[d], size, owner, 1 if d == 0 else nz - 1)))

    def sib(rel, x, src, size, who):
        at = rows_of(2 * lax.rem(z + rel, nz) + who)
        return pltpu.make_async_remote_copy(
            src_ref=wt.at[pl.ds(src, size), at], dst_ref=wt.at[pl.ds(src, size), at],
            send_sem=sib_s.at[rel, x], recv_sem=sib_r.at[rel, x],
            device_id=(sib_id, v), device_id_type=MESH,
        )

    start = lambda copy: copy.start()
    sent = lambda copy: copy.wait_send()

    @pl.loop(1, far + 1)
    def _(k):
        for d in (0, 1):
            direct(d, far + 1 - k, start)

    @pl.loop(0, arc - 1)
    def _(p):
        for d in (0, 1):
            onward(d, p, 1, start)

    @pl.loop(0, arc)
    def _(x):
        by_tiles(base + x, lambda src, size: sib(0, x, src, size, core).start())

    def take(d, p, e):
        owner = owner_at(d, e)
        rel = nz - e if d == 0 else e
        x = arc - 1 - p if d == 0 else p

        def act(src, size):
            ring(d, p, e, src, src, size, owner, 1).wait_recv()

            @pl.when(p < arc - 1)
            def _():
                ring(d, p + 1, e + 1, src, src - ahead[d], size, owner, 1 if d == 0 else nz - 1).start()

            sib(rel, x, src, size, core).start()

        by_tiles(place(d, p), act)

    def relay(s):
        @pl.loop(0, far)
        def _(k):
            for d in (0, 1):
                take(d, s - 1, far + s - 1 - k)

        @pl.loop(s, arc)
        def _(p):
            for d in (0, 1):
                take(d, p, s)

    pairs = gl.shape[1] // 256

    def tile(i):
        return jnp.minimum(i, n_mine - 1)

    def shard_tile(i):
        return lax.rem(tile_lo + tile(i), nt)

    def chip_rows(rel):
        return pl.ds(pl.multiple_of(lax.rem(z + rel, nz) * ck, ck), ck)

    def ready(rel, low, high):
        @pl.loop(low, high)
        def _(x):
            by_tiles(base + x, lambda src, size: sib(rel, x, src, size, 1 - core).wait_recv())

    def accumulate(rels, first, low=0, high=pairs):
        lhs = jnp.concatenate(
            [hall[:, :, chip_rows(rel)].reshape(rows_n, ck) for rel in rels], axis=1
        )

        @pl.loop(low, high)
        def _(p):
            at = pl.ds(pl.multiple_of(p * 256, 256), 256)
            two = [
                jnp.concatenate([wt[tile(2 * p + s), chip_rows(rel)] for rel in rels], axis=0)
                for s in (0, 1)
            ]
            got = jnp.dot(lhs, jnp.concatenate(two, axis=1), preferred_element_type=f32)
            if first:
                logits[:, at] = got
            else:
                logits[:, at] += got

    def hb_copy(k, size, peer, at_v):
        at = pl.ds(pl.multiple_of(at_v * dcol, 128), dcol)
        return pltpu.make_async_remote_copy(
            src_ref=hx.at[both(k, size)], dst_ref=hall.at[(*both(k, size), at)],
            send_sem=hb_s.at[k, peer], recv_sem=hb_r.at[k, at_v],
            device_id=(dp, peer), device_id_type=MESH,
        )

    def spread():
        for k in others:
            by_rows(k, lambda size: hx_copy(k, size, k).wait_recv())

            @pl.loop(1, nv)
            def _(j):
                peer = lax.rem(v + j, nv)
                by_rows(k, lambda size: hb_copy(k, size, peer, v).start())

            hall[pl.ds(2 * k, 2), :, mine] = hx[pl.ds(2 * k, 2)]

    def spread_done():
        for k in others:

            @pl.loop(1, nv)
            def _(j):
                peer = lax.rem(v + j, nv)
                by_rows(k, lambda size: hb_copy(k, size, peer, peer).wait_recv())

    near = min(arc - 1, far)
    begin = min(begin_at, arc)
    done = max(e for e in range(near + 1) if e == 0 or any(
        s >= begin and e < s and e in (2 * (s - begin) + 1, 2 * (s - begin) + 2)
        for s in range(1, arc + 1)))
    rest = tuple(range(done + 1, nz - done))
    top_size = -(-nt // nz)
    low = -(-top_size // 2)
    high = max(low, min(
        (-(-nt * (b + arc - 1) // nz) - -(-nt * b // nz)) // 2 for b in range(nz)))

    @pl.loop(1, arc + 1)
    def _(s):
        relay(s)
        pl.when(s == min(spread_at, arc - 1))(spread)

        @pl.when(s == begin)
        def _():
            spread_done()
            ready(0, 0, arc)
            accumulate((0,), True)

        for extra in range(2):
            e = 2 * (s - begin) + 1 + extra

            @pl.when((s >= begin) & (e <= near) & (e < s))
            def _():
                ready(nz - e, 0, arc)
                ready(e, 0, arc)
                accumulate((nz - e, e), False)

        @pl.when(s == max(arc - 1, begin))
        def _():
            if low < high:
                for rel in rest:
                    ready(rel, 1, arc - 1)
                accumulate(rest, False, low, high)

    for rel in rest:
        if low < high:
            ready(rel, 0, 1)
            ready(rel, arc - 1, arc)
        else:
            ready(rel, 0, arc)
    accumulate(rest, False, 0, low)
    accumulate(rest, False, high, pairs)

    for k in others:
        tg_copy(k, k).wait_recv()
    tl = []
    for k in range(groups):
        wide = jnp.broadcast_to(tg[k, 0:1, :], (128, 256))
        tl.append(jnp.transpose(wide)[0:seg, 0:1])
    local_t = jnp.concatenate(tl, axis=0) - (v * cols).astype(f32)

    def cut(p):
        return pl.ds(pl.multiple_of(p * 256, 256), 256)

    def ids(p):
        lane = lax.broadcasted_iota(jnp.int32, (1, 256), 1)
        low = lane < 128
        at = jnp.where(low, shard_tile(2 * p) * 128 + lane, shard_tile(2 * p + 1) * 128 + lane - 128)
        return at.astype(f32), lane + p * 256 < n_mine * 128

    def highest(p, top):
        ok = ids(p)[1]
        return jnp.maximum(top, jnp.max(jnp.where(ok, logits[:, cut(p)], -jnp.inf), axis=1, keepdims=True))

    peak = lax.fori_loop(0, pairs, highest, jnp.full((rows_n, 1), -jnp.inf, f32))

    def tally(p, carry):
        total, target = carry
        at, ok = ids(p)
        part = logits[:, cut(p)]
        total = total + jnp.sum(jnp.where(ok, jnp.exp(part - peak), 0.0), axis=1, keepdims=True)
        hit = (local_t == at) & ok
        target = target + jnp.sum(jnp.where(hit, part, 0.0), axis=1, keepdims=True)
        return total, target

    zero = jnp.zeros((rows_n, 1), f32)
    total, target = lax.fori_loop(0, pairs, tally, (zero, zero))
    lane = lax.broadcasted_iota(jnp.int32, (rows_n, 128), 1)
    table = jnp.where(lane == 0, peak, jnp.where(lane == 1, total, jnp.where(lane == 2, target, 0.0)))
    if lanes > rows_n:
        table = jnp.concatenate([table, jnp.zeros((lanes - rows_n, 128), f32)], axis=0)
    zstat[kz] = jnp.transpose(table)[0:8, :]

    def zst_copy(slot, to):
        return pltpu.make_async_remote_copy(
            src_ref=zstat.at[slot], dst_ref=zstat.at[slot],
            send_sem=zst_s.at[to], recv_sem=zst_r.at[slot],
            device_id=(plane_dev(to), v), device_id_type=MESH,
        )

    for to in others:
        zst_copy(kz, to).start()

    @pl.loop(1, far + 1)
    def _(e):
        for d in (0, 1):
            direct(d, e, sent)

    @pl.loop(0, arc - 1)
    def _(p):
        @pl.loop(1, far + p + 2)
        def _(e):
            for d in (0, 1):
                onward(d, p, e, sent)

    @pl.loop(0, arc)
    def _(x):
        @pl.loop(0, nz)
        def _(rel):
            by_tiles(base + x, lambda src, size: sib(rel, x, src, size, core).wait_send())

    for to in others:
        by_rows(kz, lambda size: hx_copy(kz, size, to).wait_send())
        tg_copy(kz, to).wait_send()

    @pl.loop(1, nv)
    def _(j):
        peer = lax.rem(v + j, nv)
        for k in others:
            by_rows(k, lambda size: hb_copy(k, size, peer, v).wait_send())

    for k in others:
        zst_copy(k, k).wait_recv()

    def joined(ref, n):
        top = ref[0, 0:1, :]
        for k in range(1, n):
            top = jnp.maximum(top, ref[k, 0:1, :])
        whole, hit = jnp.zeros_like(top), jnp.zeros_like(top)
        for k in range(n):
            whole = whole + ref[k, 1:2, :] * jnp.exp(ref[k, 0:1, :] - top)
            hit = hit + ref[k, 2:3, :]
        return top, whole, hit

    top, whole, hit = joined(zstat, groups)
    r8 = lax.broadcasted_iota(jnp.int32, (8, lanes), 0)
    stat[v] = jnp.where(r8 == 0, top, jnp.where(r8 == 1, whole, jnp.where(r8 == 2, hit, 0.0)))

    def stat_copy(peer, slot):
        return pltpu.make_async_remote_copy(
            src_ref=stat.at[slot], dst_ref=stat.at[slot],
            send_sem=stat_s.at[peer], recv_sem=stat_r.at[slot],
            device_id=(dp, peer), device_id_type=MESH,
        )

    @pl.loop(1, nv)
    def _(k):
        stat_copy(lax.rem(v + k, nv), v).start()

    @pl.loop(1, nv)
    def _(k):
        peer = lax.rem(v + k, nv)
        stat_copy(peer, peer).wait_recv()

    top, whole, hit = joined(stat, nv)
    log_total = top + jnp.log(whole)
    token = hit - log_total
    lt_col = jnp.transpose(jnp.broadcast_to(log_total, (128, lanes)))[0:rows_n, 0:1]

    @pl.loop(0, pairs)
    def _(p):
        at, ok = ids(p)
        soft = jnp.exp(logits[:, cut(p)] - lt_col)
        onehot = (local_t == at).astype(f32)
        gl[:, cut(p)] = jnp.where(ok, onehot - soft, 0.0).astype(bf16)

    def g_copy(k, size, peer, slot):
        return pltpu.make_async_remote_copy(
            src_ref=gsend.at[(peer, *both(k, size))], dst_ref=grecv.at[(slot, *both(k, size))],
            send_sem=g_s.at[k, peer], recv_sem=g_r.at[k, slot],
            device_id=(dp, peer), device_id_type=MESH,
        )

    npair = nv // 2

    @pl.loop(0, npair)
    def _(i):
        q = lax.rem(lax.div(v, 2) + i + 1, npair)
        at = pl.ds(pl.multiple_of(q * 2 * dcol, 128), 2 * dcol)
        got = jnp.zeros((rows_n, 2 * dcol), f32)
        for p in range(pairs):
            rhs = jnp.concatenate([wt[tile(2 * p), at], wt[tile(2 * p + 1), at]], axis=1)
            got = got + lax.dot_general(
                gl[:, p * 256 : (p + 1) * 256], rhs, (((1,), (1,)), ((), ())),
                preferred_element_type=f32,
            )
        got = got.astype(bf16).reshape(2 * groups, window, 2 * dcol)
        for side in (0, 1):
            peer = 2 * q + side
            gsend[peer] = got[:, :, side * dcol : (side + 1) * dcol]

            @pl.when(peer != v)
            def _():
                for k in others:
                    by_rows(k, lambda size: g_copy(k, size, peer, v).start())

    @pl.loop(2, nv + 2)
    def _(i):
        peer = lax.rem(2 * lax.div(v, 2) + i, nv)

        @pl.when(peer != v)
        def _():
            by_rows(kz, lambda size: g_copy(kz, size, peer, v).start())

    spot = lax.broadcasted_iota(jnp.int32, (1, lanes), 1) - kz * seg
    sums = []
    for m in (0, 1):
        inside = (spot >= m * window) & (spot < m * window + lens[m])
        sums.append(jnp.sum(jnp.where(inside, token, 0.0), axis=1, keepdims=True))
    refs = [refs_ref[0:1, m : m + 1] for m in (0, 1)]
    count = (lens[0] + lens[1]).astype(f32)
    ml = lax.broadcasted_iota(jnp.int32, (8, 128), 1)
    mr = lax.broadcasted_iota(jnp.int32, (8, 128), 0)
    word = jnp.zeros((8, 128), f32)
    for at, value in enumerate((sums[0], sums[1], refs[0], refs[1], count)):
        word = jnp.where((ml == at) & (mr == 0), value, word)
    msg[dp] = word

    def msg_copy(peer, slot):
        return pltpu.make_async_remote_copy(
            src_ref=msg.at[slot], dst_ref=msg.at[slot],
            send_sem=msg_s.at[peer], recv_sem=msg_r.at[slot],
            device_id=(peer, v), device_id_type=MESH,
        )

    @pl.loop(1, dp_n)
    def _(k):
        msg_copy(lax.rem(dp + k, dp_n), dp).start()

    def summed(k):
        @pl.loop(1, nv)
        def _(j):
            peer = lax.rem(v + j, nv)
            by_rows(k, lambda size: g_copy(k, size, peer, peer).wait_recv())

        return lax.fori_loop(
            1, nv,
            lambda j, acc: acc + grecv[lax.rem(v + j, nv), pl.ds(2 * k, 2)].astype(f32),
            gsend[v, pl.ds(2 * k, 2)].astype(f32),
        )

    def f_copy(k, size, slot, to):
        return pltpu.make_async_remote_copy(
            src_ref=fsend.at[both(k, size)], dst_ref=frecv.at[both(slot, size)],
            send_sem=f_s.at[k], recv_sem=f_r.at[slot],
            device_id=(plane_dev(to), v), device_id_type=MESH,
        )

    for k in others:
        fsend[pl.ds(2 * k, 2)] = summed(k).astype(bf16)
        by_rows(k, lambda size: f_copy(k, size, kz, k).start())

    @pl.loop(1, dp_n)
    def _(k):
        peer = lax.rem(dp + k, dp_n)
        msg_copy(peer, peer).wait_recv()

    board = jnp.sum(msg[...], axis=1)
    mean_length = jnp.sum(board[:, 4:5], axis=0, keepdims=True) / float(2 * dp_n)
    who = lax.broadcasted_iota(jnp.int32, (dp_n, 1), 0)
    weights = []
    loss_lane = lax.broadcasted_iota(jnp.int32, (1, 2), 1)
    losses = jnp.zeros((1, 2), f32)
    for m in (0, 1):
        gaps = board[:, m : m + 1] / mean_length - board[:, 2 + m : 3 + m]
        own_gap = sums[m] / mean_length - refs[m]
        partner = partner_ref[0:1, m : m + 1]
        partner_gap = jnp.sum(jnp.where(who == partner, gaps, 0.0), axis=0, keepdims=True)
        sign = jnp.where(dp < partner, 1.0, -1.0)
        margin = margin_beta * sign * (own_gap - partner_gap)
        small = jnp.exp(-jnp.abs(margin))
        loss = jnp.maximum(-margin, 0.0) + jnp.log1p(small)
        sig = jnp.where(margin >= 0, small, 1.0) / (1.0 + small)
        weights.append(-loss_scale * margin_beta * sign * sig / mean_length)
        losses = jnp.where(loss_lane == m, loss, losses)
    loss_ref[...] = losses

    grads = summed(kz)

    for to in others:
        by_rows(to, lambda size: f_copy(to, size, kz, to).wait_send())
        zst_copy(kz, to).wait_send()

    @pl.loop(1, nv)
    def _(j):
        peer = lax.rem(v + j, nv)
        stat_copy(peer, v).wait_send()
        for k in [kz] + others:
            by_rows(k, lambda size: g_copy(k, size, peer, v).wait_send())

    @pl.loop(1, dp_n)
    def _(k):
        msg_copy(lax.rem(dp + k, dp_n), dp).wait_send()

    for k in others:
        by_rows(kz, lambda size: f_copy(k, size, k, k).wait_recv())
        grads = grads + frecv[pl.ds(2 * k, 2)].astype(f32)
    for m in (0, 1):
        part = jnp.where(masks[m], grads[m] * weights[m], 0.0)
        pos = lax.broadcasted_iota(jnp.int32, (128, window), 0)
        row = lax.broadcasted_iota(jnp.int32, (128, window), 1)
        back = (pos == row + starts[m]).astype(f32)
        grad_ref[m] = jnp.dot(
            back, part, preferred_element_type=f32, precision=lax.Precision.HIGHEST
        )


def solution(mesh):
    dp_n, nv = mesh.shape["dp"], mesh.shape["vocab"]
    nz = dp_n // 2
    arc = nz // groups
    far = (nz - arc) // 2

    def body(hidden, out_weight, targets, prompt_start, response_len, partner, ref_scores):
        micro, seqs, length, depth = hidden.shape
        kr, cols = out_weight.shape
        nt = cols // 128
        most = max(-(-nt * (z + arc) // nz) - -(-nt * z // nz) for z in range(nz))
        wide = -(-most // 2) * 256
        seg = 2 * window
        rows_n = groups * seg
        lanes = -(-rows_n // 128) * 128
        dcol = depth // nv
        f32, bf16, i32 = jnp.float32, jnp.bfloat16, jnp.int32
        vm = pl.BlockSpec(memory_space=pltpu.VMEM)
        hbm = pl.BlockSpec(memory_space=pltpu.HBM)
        dma = pltpu.SemaphoreType.DMA
        mem = pltpu.VMEM
        loss, grad = pl.pallas_call(
            functools.partial(kernel, dp_n, nv),
            out_shape=(
                jax.ShapeDtypeStruct((1, micro), f32),
                jax.ShapeDtypeStruct((micro, length, dcol), f32),
            ),
            in_specs=[hbm] * 7,
            out_specs=(vm, vm),
            scratch_shapes=[
                mem((micro * length, depth), bf16),
                mem((micro, length), i32),
                mem((1, micro), i32), mem((1, micro), i32), mem((1, micro), i32),
                mem((1, micro), f32),
                mem((nt, depth, 128), bf16),
                mem((2 * groups, window, depth), bf16),
                mem((2 * groups, window, dcol), bf16),
                mem((groups, 8, 256), f32),
                mem((rows_n, wide), f32),
                mem((rows_n, wide), bf16),
                mem((nv, 8, lanes), f32),
                mem((groups, 8, lanes), f32),
                mem((nv, 2 * groups, window, dcol), bf16),
                mem((nv, 2 * groups, window, dcol), bf16),
                mem((2 * groups, window, dcol), bf16),
                mem((2 * groups, window, dcol), bf16),
                mem((dp_n, 8, 128), f32),
                dma((6,)), dma((nt,)),
                dma((2, arc, far + arc)), dma((2, arc, far + arc)),
                dma((nz, arc)), dma((nz, arc)),
                dma((groups,)), dma((groups,)),
                dma((groups,)), dma((groups,)),
                dma((groups, nv)), dma((groups, nv)),
                dma((groups,)), dma((groups,)),
                dma((nv,)), dma((nv,)),
                dma((dp_n,)), dma((dp_n,)),
                dma((groups, nv)), dma((groups, nv)),
                dma((groups,)), dma((groups,)),
            ],
            compiler_params=pltpu.CompilerParams(
                collective_id=0, has_side_effects=True, vmem_limit_bytes=56 * 1024 * 1024
            ),
        )(
            hidden.reshape(micro * length, depth),
            out_weight,
            targets.reshape(micro, length),
            prompt_start.reshape(1, micro),
            response_len.reshape(1, micro),
            partner.reshape(1, micro),
            ref_scores.reshape(1, micro),
        )
        return loss.reshape(micro, seqs), grad.reshape(micro, seqs, length, dcol)

    return jax.shard_map(
        body,
        mesh=mesh,
        in_specs=(
            P(None, "dp", None, None),
            P("dp", "vocab"),
            P(None, "dp", None),
            P(None, "dp"),
            P(None, "dp"),
            P(None, "dp"),
            P(None, "dp"),
        ),
        out_specs=(P(None, "dp"), P(None, "dp", None, "vocab")),
        check_vma=False,
    )
```

```python
import functools

import jax
import jax.numpy as jnp
from jax import lax
from jax.experimental import pallas as pl
from jax.experimental.pallas import tpu as pltpu
from jax.sharding import PartitionSpec as P

MESH = pl.DeviceIdType.MESH
margin_beta = 0.1
loss_scale = 65536.0
window = 80
groups = 2
spread_at = 2
begin_at = 4


def kernel(
    dp_n, nv, h_hbm, w_hbm, t_hbm, start_hbm, len_hbm, partner_hbm, refs_hbm,
    loss_ref, grad_ref,
    h_ref, t_ref, start_ref, len_ref, partner_ref, refs_ref,
    wt, hall, hx, tg, logits, gl, stat, zstat, gsend, grecv, fsend, frecv, msg,
    oh, osend, orecv, osum, oback, columns,
    in_sem, own_sem, ring_s, ring_r, sib_s, sib_r, hx_s, hx_r, tg_s, tg_r, hb_s, hb_r,
    zst_s, zst_r, stat_s, stat_r, msg_s, msg_r, g_s, g_r, f_s, f_r, o_s, o_r, fo_s, fo_r,
):
    f32, bf16 = jnp.float32, jnp.bfloat16
    dp, v = lax.axis_index("dp"), lax.axis_index("vocab")
    nz = dp_n // 2
    z, core = lax.div(dp, 2), lax.rem(dp, 2)
    sib_id = dp + 1 - 2 * core
    kr, cols = w_hbm.shape
    depth = hall.shape[2]
    dcol = depth // nv
    nt = cols // 128
    arc = nz // groups
    far = (nz - arc) // 2
    seg = 2 * window
    rows_n = groups * seg
    ck = 2 * kr
    lanes = zstat.shape[2]
    kz, zlow = lax.div(z, arc), lax.rem(z, arc)

    inputs = [
        pltpu.make_async_copy(src, dst, in_sem.at[k])
        for k, (src, dst) in enumerate((
            (h_hbm, h_ref), (t_hbm, t_ref), (start_hbm, start_ref), (len_hbm, len_ref),
            (partner_hbm, partner_ref), (refs_hbm, refs_ref),
        ))
    ]
    for copy in inputs:
        copy.start()

    def first_tile(p):
        return lax.div(nt * p + nz - 1, nz)

    base = z + 2 * nz - arc + 1
    tile_base = first_tile(base)
    tile_lo = lax.rem(tile_base, nt)
    n_mine = first_tile(base + arc) - tile_base

    def rows_of(owner):
        return pl.ds(pl.multiple_of(owner * kr, kr), kr)

    def own_copy(t):
        at = pl.ds(pl.multiple_of(t * 128, 128), 128)
        slot = lax.rem(t + nt - tile_lo, nt)
        return pltpu.make_async_copy(w_hbm.at[:, at], wt.at[slot, rows_of(dp)], own_sem.at[t])

    @pl.loop(0, nt)
    def _(t):
        own_copy(t).start()

    bar = pltpu.get_barrier_semaphore()

    @pl.loop(1, dp_n)
    def _(k):
        pl.semaphore_signal(bar, inc=1, device_id=(lax.rem(dp + k, dp_n), v), device_id_type=MESH)

    @pl.loop(1, nv)
    def _(k):
        pl.semaphore_signal(bar, inc=1, device_id=(dp, lax.rem(v + k, nv)), device_id_type=MESH)

    for copy in inputs:
        copy.wait()

    def seg_rows(k):
        return pl.ds(pl.multiple_of(k * seg, 16), seg)

    starts = [start_ref[0:1, m : m + 1] for m in (0, 1)]
    lens = [len_ref[0:1, m : m + 1] for m in (0, 1)]
    tcols, masks = [], []
    for m in (0, 1):
        pos = lax.broadcasted_iota(jnp.int32, (window, 128), 1)
        row = lax.broadcasted_iota(jnp.int32, (window, 128), 0)
        pick_f = (pos == row + starts[m]).astype(f32)
        tcols.append(jnp.sum(pick_f * t_ref[m : m + 1, :].astype(f32), axis=1, keepdims=True))
        masks.append(lax.broadcasted_iota(jnp.int32, (window, 1), 0) < lens[m])
        sel = pick_f.astype(bf16)

        @pl.loop(0, depth // 512)
        def _(c):
            at = pl.ds(pl.multiple_of(c * 512, 512), 512)
            got = jnp.dot(sel, h_ref[m * 128 : m * 128 + 128, at], preferred_element_type=f32)
            hall[2 * kz + m, :, at] = got.astype(bf16)

    tcol = jnp.concatenate(tcols + [jnp.zeros((256 - seg, 1), f32)], axis=0)
    tg[kz] = jnp.transpose(jnp.broadcast_to(tcol, (256, 128)))[0:8, :]

    @pl.loop(0, nt)
    def _(t):
        own_copy(t).wait()

    pl.semaphore_wait(bar, dp_n - 1 + nv - 1)

    def tall(k):
        s = 2 * (zlow + k * arc) + core
        return lax.div(31 + lax.div(64 * (s + 1), dp_n), 16)

    def by_rows(k, act):
        for size in (2, 3, 4, 5):
            pl.when(tall(k) == size)(functools.partial(act, 16 * size))

    def plane_dev(k):
        return 2 * (zlow + k * arc) + core

    mine = pl.ds(pl.multiple_of(v * dcol, 128), dcol)

    def both(k, size):
        return pl.ds(2 * k, 2), pl.ds(0, size)

    def hx_copy(slot, size, to):
        return pltpu.make_async_remote_copy(
            src_ref=hall.at[(*both(slot, size), mine)], dst_ref=hx.at[both(slot, size)],
            send_sem=hx_s.at[to], recv_sem=hx_r.at[slot],
            device_id=(plane_dev(to), v), device_id_type=MESH,
        )

    def tg_copy(slot, to):
        return pltpu.make_async_remote_copy(
            src_ref=tg.at[slot], dst_ref=tg.at[slot],
            send_sem=tg_s.at[to], recv_sem=tg_r.at[slot],
            device_id=(plane_dev(to), v), device_id_type=MESH,
        )

    others = [lax.rem(kz + k, groups) for k in range(1, groups)]
    for to in others:
        by_rows(kz, lambda size: hx_copy(kz, size, to).start())
        tg_copy(kz, to).start()

    sizes = range(nt // nz, -(-nt // nz) + 1)

    def by_tiles(x, act):
        t0 = first_tile(x)
        n = first_tile(x + 1) - t0
        for size in sizes:
            pl.when(n == size)(functools.partial(act, t0 - tile_base, size))

    def ring(d, p, e, src, dst, size, owner, step):
        to = lax.rem(dp + 2 * step, dp_n)
        at = rows_of(owner)
        return pltpu.make_async_remote_copy(
            src_ref=wt.at[pl.ds(src, size), at], dst_ref=wt.at[pl.ds(dst, size), at],
            send_sem=ring_s.at[d, p, e], recv_sem=ring_r.at[d, p, e],
            device_id=(to, v), device_id_type=MESH,
        )

    ahead = (first_tile(base + 1) - tile_base, first_tile(base - 1) - tile_base)

    def place(d, p):
        return base + arc - 1 - p if d == 0 else base + p

    def owner_at(d, e):
        return 2 * lax.rem(z + (nz - e if d == 0 else e), nz) + core

    def direct(d, e, act):
        if d == 0:
            shift = first_tile(base + e) - tile_base
            by_tiles(base + e + arc - 1, lambda src, size: act(
                ring(0, 0, e, src, src - shift, size, dp, e)))
        else:
            by_tiles(base + nz - e, lambda src, size: act(
                ring(1, 0, e, src, 0, size, dp, nz - e)))

    def onward(d, p, e, act):
        owner = owner_at(d, e - 1)
        by_tiles(place(d, p), lambda src, size: act(
            ring(d, p + 1, e, src, src - ahead[d], size, owner, 1 if d == 0 else nz - 1)))

    def sib(rel, x, src, size, who):
        at = rows_of(2 * lax.rem(z + rel, nz) + who)
        return pltpu.make_async_remote_copy(
            src_ref=wt.at[pl.ds(src, size), at], dst_ref=wt.at[pl.ds(src, size), at],
            send_sem=sib_s.at[rel, x], recv_sem=sib_r.at[rel, x],
            device_id=(sib_id, v), device_id_type=MESH,
        )

    start = lambda copy: copy.start()
    sent = lambda copy: copy.wait_send()

    @pl.loop(1, far + 1)
    def _(k):
        for d in (0, 1):
            direct(d, far + 1 - k, start)

    @pl.loop(0, arc - 1)
    def _(p):
        for d in (0, 1):
            onward(d, p, 1, start)

    @pl.loop(0, arc)
    def _(x):
        by_tiles(base + x, lambda src, size: sib(0, x, src, size, core).start())

    def take(d, p, e):
        owner = owner_at(d, e)
        rel = nz - e if d == 0 else e
        x = arc - 1 - p if d == 0 else p

        def act(src, size):
            ring(d, p, e, src, src, size, owner, 1).wait_recv()

            @pl.when(p < arc - 1)
            def _():
                ring(d, p + 1, e + 1, src, src - ahead[d], size, owner, 1 if d == 0 else nz - 1).start()

            sib(rel, x, src, size, core).start()

        by_tiles(place(d, p), act)

    def relay(s):
        @pl.loop(0, far)
        def _(k):
            for d in (0, 1):
                take(d, s - 1, far + s - 1 - k)

        @pl.loop(s, arc)
        def _(p):
            for d in (0, 1):
                take(d, p, s)

    pairs = gl.shape[1] // 256

    def tile(i):
        return jnp.minimum(i, n_mine - 1)

    def shard_tile(i):
        return lax.rem(tile_lo + tile(i), nt)

    def chip_rows(rel):
        return pl.ds(pl.multiple_of(lax.rem(z + rel, nz) * ck, ck), ck)

    def ready(rel, low, high):
        @pl.loop(low, high)
        def _(x):
            by_tiles(base + x, lambda src, size: sib(rel, x, src, size, 1 - core).wait_recv())

    def accumulate(rels, first, low=0, high=pairs):
        lhs = jnp.concatenate(
            [hall[:, :, chip_rows(rel)].reshape(rows_n, ck) for rel in rels], axis=1
        )

        @pl.loop(low, high)
        def _(p):
            at = pl.ds(pl.multiple_of(p * 256, 256), 256)
            two = [
                jnp.concatenate([wt[tile(2 * p + s), chip_rows(rel)] for rel in rels], axis=0)
                for s in (0, 1)
            ]
            got = jnp.dot(lhs, jnp.concatenate(two, axis=1), preferred_element_type=f32)
            if first:
                logits[:, at] = got
            else:
                logits[:, at] += got

    def hb_copy(k, size, peer, at_v):
        at = pl.ds(pl.multiple_of(at_v * dcol, 128), dcol)
        return pltpu.make_async_remote_copy(
            src_ref=hx.at[both(k, size)], dst_ref=hall.at[(*both(k, size), at)],
            send_sem=hb_s.at[k, peer], recv_sem=hb_r.at[k, at_v],
            device_id=(dp, peer), device_id_type=MESH,
        )

    def spread():
        for k in others:
            by_rows(k, lambda size: hx_copy(k, size, k).wait_recv())

            @pl.loop(1, nv)
            def _(j):
                peer = lax.rem(v + j, nv)
                by_rows(k, lambda size: hb_copy(k, size, peer, v).start())

            hall[pl.ds(2 * k, 2), :, mine] = hx[pl.ds(2 * k, 2)]

    def spread_done():
        for k in others:

            @pl.loop(1, nv)
            def _(j):
                peer = lax.rem(v + j, nv)
                by_rows(k, lambda size: hb_copy(k, size, peer, peer).wait_recv())

    def local_targets():
        tl = []
        for k in range(groups):
            wide = jnp.broadcast_to(tg[k, 0:1, :], (128, 256))
            tl.append(jnp.transpose(wide)[0:seg, 0:1])
        return jnp.concatenate(tl, axis=0) - (v * cols).astype(f32)

    def cut(p):
        return pl.ds(pl.multiple_of(p * 256, 256), 256)

    def ids(p):
        lane = lax.broadcasted_iota(jnp.int32, (1, 256), 1)
        low = lane < 128
        at = jnp.where(low, shard_tile(2 * p) * 128 + lane, shard_tile(2 * p + 1) * 128 + lane - 128)
        return at.astype(f32), lane + p * 256 < n_mine * 128

    def find_targets():
        for k in others:
            tg_copy(k, k).wait_recv()
        local = local_targets()

        @pl.loop(0, pairs)
        def _(p):
            at, ok = ids(p)
            oh[:, cut(p)] = ((local == at) & ok).astype(f32).astype(bf16)

    def o_copy(k, size, peer, slot):
        return pltpu.make_async_remote_copy(
            src_ref=osend.at[(peer, *both(k, size))], dst_ref=orecv.at[(slot, *both(k, size))],
            send_sem=o_s.at[k, peer], recv_sem=o_r.at[k, slot],
            device_id=(dp, peer), device_id_type=MESH,
        )

    npair = nv // 2

    def blocks(lhs, out, send):
        @pl.loop(0, npair)
        def _(i):
            q = lax.rem(lax.div(v, 2) + i + 1, npair)
            at = pl.ds(pl.multiple_of(q * 2 * dcol, 128), 2 * dcol)
            got = jnp.zeros((rows_n, 2 * dcol), f32)
            for p in range(pairs):
                rhs = jnp.concatenate([wt[tile(2 * p), at], wt[tile(2 * p + 1), at]], axis=1)
                got = got + lax.dot_general(
                    lhs[:, p * 256 : (p + 1) * 256], rhs, (((1,), (1,)), ((), ())),
                    preferred_element_type=f32,
                )
            got = got.astype(bf16).reshape(2 * groups, window, 2 * dcol)
            for side in (0, 1):
                peer = 2 * q + side
                out[peer] = got[:, :, side * dcol : (side + 1) * dcol]
                pl.when(peer != v)(functools.partial(send, peer))

    near = min(arc - 1, far)
    begin = min(begin_at, arc)
    done = max(e for e in range(near + 1) if e == 0 or any(
        s >= begin and e < s and e in (2 * (s - begin) + 1, 2 * (s - begin) + 2)
        for s in range(1, arc + 1)))
    rest = tuple(range(done + 1, nz - done))
    top_size = -(-nt // nz)
    low = -(-top_size // 2)
    high = max(low, min(
        (-(-nt * (b + arc - 1) // nz) - -(-nt * b // nz)) // 2 for b in range(nz)))

    @pl.loop(1, arc + 1)
    def _(s):
        relay(s)
        pl.when(s == min(spread_at, arc - 1))(spread)

        @pl.when(s == begin)
        def _():
            spread_done()
            ready(0, 0, arc)
            accumulate((0,), True)
            find_targets()

        for extra in range(2):
            e = 2 * (s - begin) + 1 + extra

            @pl.when((s >= begin) & (e <= near) & (e < s))
            def _():
                ready(nz - e, 0, arc)
                ready(e, 0, arc)
                accumulate((nz - e, e), False)

        @pl.when(s == max(arc - 1, begin))
        def _():
            if low < high:
                for rel in rest:
                    ready(rel, 1, arc - 1)
                accumulate(rest, False, low, high)

    for rel in rest:
        if low < high:
            ready(rel, 0, 1)
            ready(rel, arc - 1, arc)
        else:
            ready(rel, 0, arc)
    accumulate(rest, False, 0, low)
    accumulate(rest, False, high, pairs)

    local_t = local_targets()

    def highest(p, top):
        ok = ids(p)[1]
        return jnp.maximum(top, jnp.max(jnp.where(ok, logits[:, cut(p)], -jnp.inf), axis=1, keepdims=True))

    peak = lax.fori_loop(0, pairs, highest, jnp.full((rows_n, 1), -jnp.inf, f32))

    def tally(p, carry):
        total, target = carry
        at, ok = ids(p)
        part = logits[:, cut(p)]
        hit = (local_t == at) & ok
        rest_of = jnp.where(ok & (local_t != at), jnp.exp(part - peak), 0.0)
        total = total + jnp.sum(rest_of, axis=1, keepdims=True)
        target = target + jnp.sum(jnp.where(hit, part, 0.0), axis=1, keepdims=True)
        return total, target

    zero = jnp.zeros((rows_n, 1), f32)
    total, target = lax.fori_loop(0, pairs, tally, (zero, zero))
    lane = lax.broadcasted_iota(jnp.int32, (rows_n, 128), 1)
    table = jnp.where(lane == 0, peak, jnp.where(lane == 1, total, jnp.where(lane == 2, target, 0.0)))
    if lanes > rows_n:
        table = jnp.concatenate([table, jnp.zeros((lanes - rows_n, 128), f32)], axis=0)
    stat[v] = jnp.transpose(table)[0:8, :]

    def stat_copy(peer, slot):
        return pltpu.make_async_remote_copy(
            src_ref=stat.at[slot], dst_ref=stat.at[slot],
            send_sem=stat_s.at[peer], recv_sem=stat_r.at[slot],
            device_id=(dp, peer), device_id_type=MESH,
        )

    @pl.loop(1, nv)
    def _(k):
        stat_copy(lax.rem(v + k, nv), v).start()

    def send_targets(peer):
        for k in others + [kz]:
            by_rows(k, lambda size: o_copy(k, size, peer, v).start())

    blocks(oh, osend, send_targets)

    @pl.loop(1, far + 1)
    def _(e):
        for d in (0, 1):
            direct(d, e, sent)

    @pl.loop(0, arc - 1)
    def _(p):
        @pl.loop(1, far + p + 2)
        def _(e):
            for d in (0, 1):
                onward(d, p, e, sent)

    @pl.loop(0, arc)
    def _(x):
        @pl.loop(0, nz)
        def _(rel):
            by_tiles(base + x, lambda src, size: sib(rel, x, src, size, core).wait_send())

    for to in others:
        by_rows(kz, lambda size: hx_copy(kz, size, to).wait_send())
        tg_copy(kz, to).wait_send()

    @pl.loop(1, nv)
    def _(j):
        peer = lax.rem(v + j, nv)
        for k in others:
            by_rows(k, lambda size: hb_copy(k, size, peer, v).wait_send())

    @pl.loop(1, nv)
    def _(k):
        peer = lax.rem(v + k, nv)
        stat_copy(peer, peer).wait_recv()

    def joined(ref, n):
        top = ref[0, 0:1, :]
        for k in range(1, n):
            top = jnp.maximum(top, ref[k, 0:1, :])
        whole, hit = jnp.zeros_like(top), jnp.zeros_like(top)
        for k in range(n):
            whole = whole + ref[k, 1:2, :] * jnp.exp(ref[k, 0:1, :] - top)
            hit = hit + ref[k, 2:3, :]
        return top, whole, hit

    top, whole, hit = joined(stat, nv)
    r8 = lax.broadcasted_iota(jnp.int32, (8, lanes), 0)
    zstat[kz] = jnp.where(r8 == 0, top, jnp.where(r8 == 1, whole, jnp.where(r8 == 2, hit, 0.0)))

    def zst_copy(slot, to):
        return pltpu.make_async_remote_copy(
            src_ref=zstat.at[slot], dst_ref=zstat.at[slot],
            send_sem=zst_s.at[to], recv_sem=zst_r.at[slot],
            device_id=(plane_dev(to), v), device_id_type=MESH,
        )

    for to in others:
        zst_copy(kz, to).start()
    top_col = jnp.transpose(jnp.broadcast_to(top, (128, lanes)))[0:rows_n, 0:1]

    @pl.loop(0, pairs)
    def _(p):
        at, ok = ids(p)
        soft = jnp.exp(logits[:, cut(p)] - top_col)
        gl[:, cut(p)] = jnp.where(ok & (local_t != at), soft, 0.0).astype(bf16)

    def g_copy(k, size, peer, slot):
        return pltpu.make_async_remote_copy(
            src_ref=gsend.at[(peer, *both(k, size))], dst_ref=grecv.at[(slot, *both(k, size))],
            send_sem=g_s.at[k, peer], recv_sem=g_r.at[k, slot],
            device_id=(dp, peer), device_id_type=MESH,
        )

    def send_partner(peer):
        for k in others:
            by_rows(k, lambda size: g_copy(k, size, peer, v).start())

    blocks(gl, gsend, send_partner)

    @pl.loop(2, nv + 2)
    def _(i):
        peer = lax.rem(2 * lax.div(v, 2) + i, nv)

        @pl.when(peer != v)
        def _():
            by_rows(kz, lambda size: g_copy(kz, size, peer, v).start())

    for k in others:
        zst_copy(k, k).wait_recv()
    top, whole, hit = joined(zstat, groups)
    every = whole + jnp.exp(hit - top)
    token = hit - top - jnp.log(every)
    r128 = lax.broadcasted_iota(jnp.int32, (128, lanes), 0)
    factors = jnp.where(r128 == 0, whole / every, 0.0)
    for at, k in enumerate([kz] + others):
        factors = jnp.where(r128 == 1 + at, jnp.exp(zstat[k, 0:1, :] - top) / every, factors)
    columns[...] = jnp.transpose(factors)

    spot = lax.broadcasted_iota(jnp.int32, (1, lanes), 1) - kz * seg
    sums = []
    for m in (0, 1):
        inside = (spot >= m * window) & (spot < m * window + lens[m])
        sums.append(jnp.sum(jnp.where(inside, token, 0.0), axis=1, keepdims=True))
    refs = [refs_ref[0:1, m : m + 1] for m in (0, 1)]
    count = (lens[0] + lens[1]).astype(f32)
    ml = lax.broadcasted_iota(jnp.int32, (8, 128), 1)
    mr = lax.broadcasted_iota(jnp.int32, (8, 128), 0)
    word = jnp.zeros((8, 128), f32)
    for at, value in enumerate((sums[0], sums[1], refs[0], refs[1], count)):
        word = jnp.where((ml == at) & (mr == 0), value, word)
    msg[dp] = word

    def msg_copy(peer, slot):
        return pltpu.make_async_remote_copy(
            src_ref=msg.at[slot], dst_ref=msg.at[slot],
            send_sem=msg_s.at[peer], recv_sem=msg_r.at[slot],
            device_id=(peer, v), device_id_type=MESH,
        )

    @pl.loop(1, dp_n)
    def _(k):
        msg_copy(lax.rem(dp + k, dp_n), dp).start()

    def summed(k, copy, out, into):
        @pl.loop(1, nv)
        def _(j):
            peer = lax.rem(v + j, nv)
            by_rows(k, lambda size: copy(k, size, peer, peer).wait_recv())

        return lax.fori_loop(
            1, nv,
            lambda j, acc: acc + into[lax.rem(v + j, nv), pl.ds(2 * k, 2)].astype(f32),
            out[v, pl.ds(2 * k, 2)].astype(f32),
        )

    def fo_copy(k, size, slot, to):
        return pltpu.make_async_remote_copy(
            src_ref=osum.at[both(k, size)], dst_ref=oback.at[both(slot, size)],
            send_sem=fo_s.at[k], recv_sem=fo_r.at[slot],
            device_id=(plane_dev(to), v), device_id_type=MESH,
        )

    def f_copy(k, size, slot, to):
        return pltpu.make_async_remote_copy(
            src_ref=fsend.at[both(k, size)], dst_ref=frecv.at[both(slot, size)],
            send_sem=f_s.at[k], recv_sem=f_r.at[slot],
            device_id=(plane_dev(to), v), device_id_type=MESH,
        )

    for k in others:
        osum[pl.ds(2 * k, 2)] = summed(k, o_copy, osend, orecv).astype(bf16)
        by_rows(k, lambda size: fo_copy(k, size, kz, k).start())
        fsend[pl.ds(2 * k, 2)] = summed(k, g_copy, gsend, grecv).astype(bf16)
        by_rows(k, lambda size: f_copy(k, size, kz, k).start())

    @pl.loop(1, dp_n)
    def _(k):
        peer = lax.rem(dp + k, dp_n)
        msg_copy(peer, peer).wait_recv()

    board = jnp.sum(msg[...], axis=1)
    mean_length = jnp.sum(board[:, 4:5], axis=0, keepdims=True) / float(2 * dp_n)
    who = lax.broadcasted_iota(jnp.int32, (dp_n, 1), 0)
    weights = []
    loss_lane = lax.broadcasted_iota(jnp.int32, (1, 2), 1)
    losses = jnp.zeros((1, 2), f32)
    for m in (0, 1):
        gaps = board[:, m : m + 1] / mean_length - board[:, 2 + m : 3 + m]
        own_gap = sums[m] / mean_length - refs[m]
        partner = partner_ref[0:1, m : m + 1]
        partner_gap = jnp.sum(jnp.where(who == partner, gaps, 0.0), axis=0, keepdims=True)
        sign = jnp.where(dp < partner, 1.0, -1.0)
        margin = margin_beta * sign * (own_gap - partner_gap)
        small = jnp.exp(-jnp.abs(margin))
        loss = jnp.maximum(-margin, 0.0) + jnp.log1p(small)
        sig = jnp.where(margin >= 0, small, 1.0) / (1.0 + small)
        weights.append(-loss_scale * margin_beta * sign * sig / mean_length)
        losses = jnp.where(loss_lane == m, loss, losses)
    loss_ref[...] = losses

    found = summed(kz, o_copy, osend, orecv)
    grads = summed(kz, g_copy, gsend, grecv)

    for to in others:
        by_rows(to, lambda size: f_copy(to, size, kz, to).wait_send())
        by_rows(to, lambda size: fo_copy(to, size, kz, to).wait_send())
        zst_copy(kz, to).wait_send()

    @pl.loop(1, nv)
    def _(j):
        peer = lax.rem(v + j, nv)
        stat_copy(peer, v).wait_send()
        for k in [kz] + others:
            by_rows(k, lambda size: g_copy(k, size, peer, v).wait_send())
            by_rows(k, lambda size: o_copy(k, size, peer, v).wait_send())

    @pl.loop(1, dp_n)
    def _(k):
        msg_copy(lax.rem(dp + k, dp_n), dp).wait_send()

    scale = columns[seg_rows(kz), :].reshape(2, window, 128)
    grads = grads * scale[:, :, 1:2]
    for at, k in enumerate(others):
        by_rows(kz, lambda size: fo_copy(k, size, k, k).wait_recv())
        found = found + oback[pl.ds(2 * k, 2)].astype(f32)
        by_rows(kz, lambda size: f_copy(k, size, k, k).wait_recv())
        grads = grads + frecv[pl.ds(2 * k, 2)].astype(f32) * scale[:, :, 2 + at : 3 + at]
    grads = found * scale[:, :, 0:1] - grads
    for m in (0, 1):
        part = jnp.where(masks[m], grads[m] * weights[m], 0.0)
        pos = lax.broadcasted_iota(jnp.int32, (128, window), 0)
        row = lax.broadcasted_iota(jnp.int32, (128, window), 1)
        back = (pos == row + starts[m]).astype(f32)
        grad_ref[m] = jnp.dot(
            back, part, preferred_element_type=f32, precision=lax.Precision.HIGHEST
        )


def solution(mesh):
    dp_n, nv = mesh.shape["dp"], mesh.shape["vocab"]
    nz = dp_n // 2
    arc = nz // groups
    far = (nz - arc) // 2

    def body(hidden, out_weight, targets, prompt_start, response_len, partner, ref_scores):
        micro, seqs, length, depth = hidden.shape
        kr, cols = out_weight.shape
        nt = cols // 128
        most = max(-(-nt * (z + arc) // nz) - -(-nt * z // nz) for z in range(nz))
        wide = -(-most // 2) * 256
        seg = 2 * window
        rows_n = groups * seg
        lanes = -(-rows_n // 128) * 128
        dcol = depth // nv
        f32, bf16, i32 = jnp.float32, jnp.bfloat16, jnp.int32
        vm = pl.BlockSpec(memory_space=pltpu.VMEM)
        hbm = pl.BlockSpec(memory_space=pltpu.HBM)
        dma = pltpu.SemaphoreType.DMA
        mem = pltpu.VMEM
        loss, grad = pl.pallas_call(
            functools.partial(kernel, dp_n, nv),
            out_shape=(
                jax.ShapeDtypeStruct((1, micro), f32),
                jax.ShapeDtypeStruct((micro, length, dcol), f32),
            ),
            in_specs=[hbm] * 7,
            out_specs=(vm, vm),
            scratch_shapes=[
                mem((micro * length, depth), bf16),
                mem((micro, length), i32),
                mem((1, micro), i32), mem((1, micro), i32), mem((1, micro), i32),
                mem((1, micro), f32),
                mem((nt, depth, 128), bf16),
                mem((2 * groups, window, depth), bf16),
                mem((2 * groups, window, dcol), bf16),
                mem((groups, 8, 256), f32),
                mem((rows_n, wide), f32),
                mem((rows_n, wide), bf16),
                mem((nv, 8, lanes), f32),
                mem((groups, 8, lanes), f32),
                mem((nv, 2 * groups, window, dcol), bf16),
                mem((nv, 2 * groups, window, dcol), bf16),
                mem((2 * groups, window, dcol), bf16),
                mem((2 * groups, window, dcol), bf16),
                mem((dp_n, 8, 128), f32),
                mem((rows_n, wide), bf16),
                mem((nv, 2 * groups, window, dcol), bf16),
                mem((nv, 2 * groups, window, dcol), bf16),
                mem((2 * groups, window, dcol), bf16),
                mem((2 * groups, window, dcol), bf16),
                mem((lanes, 128), f32),
                dma((6,)), dma((nt,)),
                dma((2, arc, far + arc)), dma((2, arc, far + arc)),
                dma((nz, arc)), dma((nz, arc)),
                dma((groups,)), dma((groups,)),
                dma((groups,)), dma((groups,)),
                dma((groups, nv)), dma((groups, nv)),
                dma((groups,)), dma((groups,)),
                dma((nv,)), dma((nv,)),
                dma((dp_n,)), dma((dp_n,)),
                dma((groups, nv)), dma((groups, nv)),
                dma((groups,)), dma((groups,)),
                dma((groups, nv)), dma((groups, nv)),
                dma((groups,)), dma((groups,)),
            ],
            compiler_params=pltpu.CompilerParams(
                collective_id=0, has_side_effects=True, vmem_limit_bytes=56 * 1024 * 1024
            ),
        )(
            hidden.reshape(micro * length, depth),
            out_weight,
            targets.reshape(micro, length),
            prompt_start.reshape(1, micro),
            response_len.reshape(1, micro),
            partner.reshape(1, micro),
            ref_scores.reshape(1, micro),
        )
        return loss.reshape(micro, seqs), grad.reshape(micro, seqs, length, dcol)

    return jax.shard_map(
        body,
        mesh=mesh,
        in_specs=(
            P(None, "dp", None, None),
            P("dp", "vocab"),
            P(None, "dp", None),
            P(None, "dp"),
            P(None, "dp"),
            P(None, "dp"),
            P(None, "dp"),
        ),
        out_specs=(P(None, "dp"), P(None, "dp", None, "vocab")),
        check_vma=False,
    )
```
